32 devices in a mesh: ctx: 4 (over x, core), exp: 4 (over z), tp: 2 (over y).
Axes of the slice: x: 2, y: 2, z: 4, core: 2. Of those that a mesh axis runs over, the one named last changes fastest.
Arguments:
- mamba_in: bfloat16 [512, 8192], P('ctx', ('exp', 'tp')), may hold values from -6 to 6
- gate_in: bfloat16 [512, 8192], P('ctx', ('exp', 'tp')), may hold values from -6 to 6
- step_size: float32 [512, 8192], P('ctx', ('exp', 'tp')), may hold values from 0 to 2
- input_proj: float32 [16, 512], P(None, 'ctx'), may hold values from -6 to 6
- output_proj: float32 [16, 512], P(None, 'ctx'), may hold values from -6 to 6
- decay_log: float32 [16, 8192], P(None, ('exp', 'tp')), may hold values from -0.7 to 0.7
- skip_gain: float32 [8192], P(('exp', 'tp')), may hold values from 0.5 to 2
- out_weight: bfloat16 [8192, 2048], P(('exp', 'tp')), may hold values from -0.0625 to 0.0625
- residual: bfloat16 [512, 2048], P('ctx', ('exp', 'tp')), may hold values from -6 to 6
- routes: int32 [512, 2], P('ctx'), may hold values from 0 to 3, all different within a row; in each aligned block of 128 rows (0 to 127, 128 to 255, ...) at most 128 rows name the same one
- norm_gain: float32 [2048], replicated, may hold values from 0.25 to 1.75
- w_gate: bfloat16 [4, 2048, 14336], P('exp', None, ('ctx', 'tp')), may hold values from -0.125 to 0.125
- w_up: bfloat16 [4, 2048, 14336], P('exp', None, ('ctx', 'tp')), may hold values from -0.125 to 0.125
- w_down: bfloat16 [4, 14336, 2048], P('exp', 'ctx', 'tp'), may hold values from -0.046875 to 0.046875
Outputs:
- expert_out: bfloat16 [4, 4, 128, 2048], P('ctx', 'exp', None, 'tp')
The draws below stay inside these ranges and needn't reach their ends.
Inputs may be any that keep to these rules, and one draw needn't show every extreme that they name: `routes`: within each aligned block of 128 positions no expert is named by more than 128 of the block's rows, a bound that some expert reaches in some block.
All inputs are finite; a program needn't handle non-finite values.
Results may differ from the reference program's by a relative error of at most 0.015.
Values may be sent and summed in bfloat16 or wider, within the bound.
A program may use at most 128 MiB of HBM per device.

```python
import math
import jax
import jax.numpy as jnp
import numpy as np
from jax import lax

D = 2048
INNER_CHANNELS = 8192
N_STATE = 16
FF = 14336
TOPK = 2
L_CH = 128
EXPERTS = 4
SEQUENCE_LENGTH = 512
CAP = 128
N_CTX = 4


def draw_step_size(key, part):
    split_random_keys = jax.random.split(key, 6)
    fast_share = 0.5
    fast_lane = jax.random.bernoulli(split_random_keys[0], fast_share, (INNER_CHANNELS,))
    slow_rate = jnp.exp(jax.random.uniform(split_random_keys[1], (INNER_CHANNELS,), jnp.float32, math.log(0.05), math.log(0.25))) / SEQUENCE_LENGTH
    fast_rate = jnp.exp(jax.random.uniform(split_random_keys[2], (INNER_CHANNELS,), jnp.float32, math.log(1.0 / 50.0), math.log(1.0 / 30.0)))
    baseline_rate = jnp.where(fast_lane, fast_rate, slow_rate)
    jitter_level = jnp.exp(jax.random.uniform(split_random_keys[3], (SEQUENCE_LENGTH, INNER_CHANNELS), jnp.float32, math.log(0.5), math.log(2.0)))
    block_multiplier = jnp.exp(jax.random.uniform(split_random_keys[4], (SEQUENCE_LENGTH // L_CH, INNER_CHANNELS), jnp.float32, math.log(0.5), math.log(2.0)))
    block_multiplier = jnp.repeat(block_multiplier, L_CH, axis=0)
    spike_keys = jax.random.split(split_random_keys[5], 2)
    spike_positions = jax.random.randint(spike_keys[0], (4,), 0, SEQUENCE_LENGTH)
    spike_mask = jnp.zeros((SEQUENCE_LENGTH,), jnp.float32).at[spike_positions].set(1.0)
    spike_length = jnp.exp(jax.random.uniform(spike_keys[1], (INNER_CHANNELS,), jnp.float32, math.log(0.25), math.log(0.7)))
    return baseline_rate[None, :] * jitter_level * block_multiplier + spike_mask[:, None] * spike_length[None, :]


def block_levels(rng, extent, pieces, low, top_value):
    gain, own = 1.0, jax.random.fold_in(rng, 6)
    for position, parts in pieces:
        steps = jnp.exp(jax.random.uniform(jax.random.fold_in(own, position), (parts,), jnp.float32, low / len(pieces), top_value / len(pieces)))
        gain = gain * jnp.repeat(steps, extent[position] // parts).reshape([-1 if axis == position else 1 for axis in range(len(extent))])
    return gain


def shared_out(key, own, number, rows, number_of, top, reach, slope):
    ranking = jax.random.permutation(key, number_of)
    packed, ordinary = portions_of(number_of, rows * top, reach, slope, True), portions_of(number_of, rows * top, reach, slope, False)
    places = jnp.arange(number_of)

    def named(tallies, rotation):
        used = int((tallies > 0).sum())
        fixed = max(1, used // 4)
        shifted = fixed + (places - fixed + rotation * (used - fixed)) % max(1, number_of - fixed)
        return jnp.zeros((number_of,), jnp.int32).at[ranking[jnp.where(places < fixed, places, shifted)]].set(jnp.asarray(tallies, jnp.int32))

    tallies = jnp.where(number % 4 == 0, named(packed, number // 4), named(ordinary, number - number // 4 - 1))
    mixed = jax.random.permutation(jax.random.fold_in(own, 3), number_of)
    donor, receiver = mixed[0:number_of // 2 * 2:2], mixed[1:number_of // 2 * 2:2]
    margin = jnp.minimum(tallies[donor] - 1, reach - tallies[receiver]) // 2
    margin = jnp.where((donor == ranking[0]) | (receiver == ranking[0]) | (tallies[receiver] == 0), 0, jnp.maximum(margin, 0))
    shifted = jax.random.randint(jax.random.fold_in(own, 4), (number_of // 2,), 0, 1 << 20) % (margin + 1)
    tallies = tallies.at[donor].add(-shifted).at[receiver].add(shifted)
    members = jnp.searchsorted(jnp.cumsum(tallies), jnp.arange(rows * top), side="right").astype(jnp.int32)
    grid = members.reshape(top, rows).T
    grid = grid[jax.random.permutation(jax.random.fold_in(own, 1), rows)]
    rotation = jax.random.randint(jax.random.fold_in(own, 2), (rows, 1), 0, top)
    return jnp.take_along_axis(grid, (jnp.arange(top)[None, :] + rotation) % top, axis=1)


def portions_of(count, total, bound, slope, full):
    portions = [(1 << 20) // math.isqrt(grade ** slope) + 1 for grade in range(1, count + 1)]
    largest = bound if full else min(bound, max(-(-total // count), total * portions[0] // sum(portions)))
    least = 1 if total - largest >= count - 1 else 0
    counts, spare = [largest] + [least] * (count - 1), total - largest - least * (count - 1)
    while spare > 0:
        movable = [i for i in range(1, count) if counts[i] < largest] or [i for i in range(1, count) if counts[i] < bound]
        pool, left = sum([portions[i] for i in movable]), spare
        for i in movable:
            addition = min(bound - counts[i], max(1, left * portions[i] // pool), spare)
            counts[i] = counts[i] + addition
            spare = spare - addition
    return np.array(counts)


def noise(own_key, shape, spread, reach, shards=(), kind=jnp.bfloat16):
    drawn = jax.random.normal(own_key, shape, jnp.float32) * spread
    if len(shards) > 0:
        drawn = block_levels(own_key, shape, shards, -0.22, 0.18) * drawn
    return jnp.clip(drawn, min=-reach, max=reach).astype(kind)


def setup_inputs(seed: int = 0) -> dict:
    streams_of = jax.random.split(jax.random.key(seed), 15)
    mamba_in = noise(streams_of[0], (SEQUENCE_LENGTH, INNER_CHANNELS), 1.0, 6.0, ((0, 4), (1, 8)))
    gate_in = noise(streams_of[1], (SEQUENCE_LENGTH, INNER_CHANNELS), 1.0, 6.0, ((0, 4), (1, 8)))
    step_size = draw_step_size(jax.random.fold_in(streams_of[14], 71), 0)
    input_proj = noise(streams_of[3], (N_STATE, SEQUENCE_LENGTH), 1.0, 6.0, ((1, 4),), jnp.float32)
    output_proj = noise(streams_of[4], (N_STATE, SEQUENCE_LENGTH), 1.0, 6.0, ((1, 4),), jnp.float32)
    decay_log = jnp.clip(jax.random.uniform(streams_of[5], (N_STATE, INNER_CHANNELS), jnp.float32, -0.7, 0.7) * block_levels(streams_of[5], (N_STATE, INNER_CHANNELS), ((1, 8),), -0.4, 0.0), -0.7, 0.7)
    skip_gain = jnp.clip(0.5 + 1.5 * jax.random.uniform(streams_of[6], (INNER_CHANNELS,), jnp.float32) ** block_levels(streams_of[6], (INNER_CHANNELS,), ((0, 8),), -0.2, 0.2), 0.5, 2.0)
    out_weight = noise(streams_of[7], (INNER_CHANNELS, D), INNER_CHANNELS ** -0.5, 0.0625, ((0, 8),))
    residual = noise(streams_of[8], (SEQUENCE_LENGTH, D), 1.0, 6.0, ((0, 4), (1, 8)))
    routes_keys = jax.random.split(jax.random.fold_in(streams_of[9], 1), SEQUENCE_LENGTH // L_CH)
    routes_turns = jax.random.permutation(jax.random.fold_in(streams_of[9], 3), SEQUENCE_LENGTH // L_CH)
    routes = jax.vmap(lambda own, number: shared_out(jax.random.fold_in(streams_of[9], 2), own, number, L_CH, EXPERTS, TOPK, CAP, 2))(routes_keys, routes_turns).reshape((SEQUENCE_LENGTH, TOPK))
    norm_gain = jnp.clip(1.0 + 0.15 * jax.random.normal(streams_of[10], (D,), jnp.float32), 0.25, 1.75)
    w_gate = noise(streams_of[11], (EXPERTS, D, FF), D ** -0.5, 0.125, ((0, 4), (2, 8)))
    w_up = noise(streams_of[12], (EXPERTS, D, FF), D ** -0.5, 0.125, ((0, 4), (2, 8)))
    w_down = noise(streams_of[13], (EXPERTS, FF, D), FF ** -0.5, 0.046875, ((0, 4), (1, 4), (2, 2)))
    return {"mamba_in": mamba_in, "gate_in": gate_in, "step_size": step_size, "input_proj": input_proj, "output_proj": output_proj, "decay_log": decay_log, "skip_gain": skip_gain, "out_weight": out_weight, "residual": residual, "routes": routes, "norm_gain": norm_gain, "w_gate": w_gate, "w_up": w_up, "w_down": w_down}


def route_rows(routes, capacity, experts):
    flattened = routes.reshape(-1)
    one_hot = (flattened[:, None] == jnp.arange(experts, dtype=jnp.int32)[None, :]).astype(jnp.int32)
    earlier = jnp.cumsum(one_hot, axis=0) - one_hot
    slot_index = lax.optimization_barrier(jnp.sum(earlier * one_hot, axis=1))
    return (flattened * capacity + slot_index).reshape(routes.shape)

def rms_scale(row_data, norm_gain):
    mean_sq = lax.optimization_barrier(jnp.mean(row_data * row_data, axis=1, keepdims=True))
    return (row_data * lax.rsqrt(mean_sq + 1e-06) * norm_gain).astype(jnp.bfloat16)

def reference(mamba_in, gate_in, step_size, input_proj, output_proj, decay_log, skip_gain, out_weight, residual, routes, norm_gain, w_gate, w_up, w_down):
    decay_rate = -jnp.exp(decay_log)
    signal = mamba_in.astype(jnp.float32)

    def advance(carried, link_item):
        step_row, signal_row, in_row, out_row = link_item
        carried = jnp.exp(step_row[None, :] * decay_rate) * carried + (step_row * signal_row)[None, :] * in_row[:, None]
        return (carried, lax.optimization_barrier(jnp.sum(out_row[:, None] * carried, axis=0)))
    start_state = jnp.zeros((N_STATE, INNER_CHANNELS), jnp.float32)
    unused, readouts = lax.scan(advance, start_state, (step_size, signal, jnp.transpose(input_proj), jnp.transpose(output_proj)))
    gated_out = ((readouts + skip_gain * signal) * jax.nn.silu(gate_in.astype(jnp.float32))).astype(jnp.bfloat16)
    mixed_rows = jnp.dot(gated_out, out_weight, preferred_element_type=jnp.float32) + residual.astype(jnp.float32)
    normed = rms_scale(mixed_rows, norm_gain)
    token_blocks = normed.reshape(N_CTX, L_CH, D)
    route_blocks = routes.reshape(N_CTX, L_CH, TOPK)

    def place(token_rows, block_routes):
        row_ids = route_rows(block_routes, CAP, EXPERTS).reshape(-1)
        copies = jnp.repeat(token_rows, TOPK, axis=0)
        return jnp.zeros((EXPERTS * CAP, D), jnp.bfloat16).at[row_ids].set(copies)
    slots = jax.vmap(place)(token_blocks, route_blocks).reshape(N_CTX, EXPERTS, CAP, D)

    def run_expert(expert_item):
        expert_rows, gate_w, up_w, down_w = expert_item
        flat_rows = expert_rows.reshape(N_CTX * CAP, D)
        gate_part = jnp.dot(flat_rows, gate_w, preferred_element_type=jnp.float32)
        up_part = jnp.dot(flat_rows, up_w, preferred_element_type=jnp.float32)
        hidden = (jax.nn.silu(gate_part) * up_part).astype(jnp.bfloat16)
        result = jnp.dot(hidden, down_w, preferred_element_type=jnp.float32).astype(jnp.bfloat16)
        return result.reshape(N_CTX, CAP, D)
    outputs = lax.map(run_expert, (jnp.transpose(slots, (1, 0, 2, 3)), w_gate, w_up, w_down))
    return jnp.transpose(outputs, (1, 0, 2, 3))
```

```python
import jax
import jax.numpy as jnp
from jax import lax
from jax.experimental import pallas as pl
from jax.experimental.pallas import tpu as pltpu
from jax.sharding import PartitionSpec as P


def prefix_2(value, axis, join, neutral):
    count, mine = (lax.axis_size(axis), lax.axis_index(axis))
    pieces = jax.tree.map(lambda part: lax.all_gather(part, axis), value)
    so_far = jax.tree.map(
        lambda part, zero: jnp.full_like(part, 0) + jnp.asarray(zero, part.dtype), value, neutral
    )

    def step(position, so_far):
        longer = join(so_far, jax.tree.map(lambda part: part[position], pieces))
        return jax.tree.map(lambda new, old: jnp.where(position < mine, new, old), longer, so_far)

    return lax.fori_loop(0, count - 1, step, so_far)


def route_rows(routes, capacity, experts):
    flattened = routes.reshape(-1)
    one_hot = (flattened[:, None] == jnp.arange(experts, dtype=jnp.int32)[None, :]).astype(
        jnp.int32
    )
    earlier = jnp.cumsum(one_hot, axis=0) - one_hot
    slot_index = jnp.sum(earlier * one_hot, axis=1)
    return (flattened * capacity + slot_index).reshape(routes.shape)


def pick_rows(row_ids, first_row, row_count):
    targets = first_row + jnp.arange(row_count, dtype=jnp.int32)
    matches = row_ids[None, :, :] == targets[:, None, None]
    return jnp.sum(matches.astype(jnp.float32), axis=2).astype(jnp.bfloat16)


def rms_scale(row_data, norm_gain):
    mean_sq = jnp.mean(row_data * row_data, axis=1, keepdims=True)
    return (row_data * lax.rsqrt(mean_sq + 1e-06) * norm_gain).astype(jnp.bfloat16)


def combine_link(earlier, later_link):
    return (earlier[0] * later_link[0], later_link[0] * earlier[1] + later_link[1])


def fold_states(rates, states, step, drive, in_ref, t):
    return tuple(
        jnp.exp(step * rate) * state + drive * in_ref[n, t]
        for n, (rate, state) in enumerate(zip(rates, states))
    )


def end_kernel(step_ref, drive_ref, rate_ref, in_ref, end_ref):
    count = rate_ref.shape[0]
    rates = [rate_ref[n] for n in range(count)]

    def advance(t, carried):
        states, total = carried
        step = step_ref[t]
        return (fold_states(rates, states, step, drive_ref[t], in_ref, t), total + step)

    zero = jnp.zeros(rate_ref.shape[1:], jnp.float32)
    states, total = lax.fori_loop(
        0, step_ref.shape[0], advance, ((zero,) * count, zero), unroll=4
    )
    for n in range(count):
        end_ref[n] = states[n]
    end_ref[count] = total


def read_kernel(
    step_ref, drive_ref, signal_ref, gate_ref, skip_ref, rate_ref, ends_ref, in_ref, out_ref, res_ref
):
    count = rate_ref.shape[0]
    mine = lax.axis_index("ctx")
    rates = [rate_ref[n] for n in range(count)]
    zero = jnp.zeros(rate_ref.shape[1:], jnp.float32)

    def join(block, states):
        total = ends_ref[block, count]
        return tuple(
            jnp.exp(total * rates[n]) * states[n] + ends_ref[block, n] for n in range(count)
        )

    incoming = lax.fori_loop(0, mine, join, (zero,) * count)
    skip = skip_ref[...]

    def advance(t, states):
        states = fold_states(rates, states, step_ref[t], drive_ref[t], in_ref, t)
        terms = [states[n] * out_ref[n, t] for n in range(count)]
        while len(terms) > 1:
            terms = [terms[i] + terms[i + 1] for i in range(0, len(terms), 2)]
        gate = gate_ref[t]
        res_ref[t] = (terms[0] + skip * signal_ref[t]) * (gate / (1.0 + jnp.exp(-gate)))
        return states

    lax.fori_loop(0, step_ref.shape[0], advance, incoming, unroll=4)


def scanned(mamba_in, gate_in, step_size, input_proj, output_proj, decay_log, skip_gain):
    length, channels = mamba_in.shape
    count = decay_log.shape[0]
    tile = (channels // 128, 128)
    signal = mamba_in.astype(jnp.float32).reshape((length,) + tile)
    gate = gate_in.astype(jnp.float32).reshape((length,) + tile)
    step = step_size.reshape((length,) + tile)
    drive = step * signal
    rate = -jnp.exp(decay_log).reshape((count,) + tile)
    vmem = pl.BlockSpec(memory_space=pltpu.VMEM)
    smem = pl.BlockSpec(memory_space=pltpu.SMEM)
    ends = pl.pallas_call(
        end_kernel,
        out_shape=jax.ShapeDtypeStruct((count + 1,) + tile, jnp.float32),
        in_specs=[vmem] * 3 + [smem],
        out_specs=vmem,
        name="end_states",
    )(step, drive, rate, input_proj)
    ends = lax.all_gather(ends, "ctx")
    gated = pl.pallas_call(
        read_kernel,
        out_shape=jax.ShapeDtypeStruct((length,) + tile, jnp.float32),
        in_specs=[vmem] * 7 + [smem] * 2,
        out_specs=vmem,
        name="read_states",
    )(step, drive, signal, gate, skip_gain.reshape(tile), rate, ends, input_proj, output_proj)
    return gated.reshape(length, channels).astype(jnp.bfloat16)


def scanned_small(mamba_in, gate_in, step_size, input_proj, output_proj, decay_log, skip_gain):
    decay_rate = -jnp.exp(decay_log)
    signal = mamba_in.astype(jnp.float32)
    decays = jnp.exp(step_size[:, None, :] * decay_rate[None, :, :])
    driving = (step_size * signal)[:, None, :] * jnp.transpose(input_proj)[:, :, None]
    cum_decay, local_state = lax.associative_scan(combine_link, (decays, driving), axis=0)
    summary = (cum_decay[-1], local_state[-1])
    identity = (jnp.ones_like(summary[0]), jnp.zeros_like(summary[1]))
    prefix = prefix_2(summary, "ctx", combine_link, identity)
    incoming = prefix[1]
    full_state = local_state + cum_decay * incoming[None, :, :]
    readout = jnp.sum(jnp.transpose(output_proj)[:, :, None] * full_state, axis=1)
    return ((readout + skip_gain * signal) * jax.nn.silu(gate_in.astype(jnp.float32))).astype(
        jnp.bfloat16
    )


def body(
    mamba_in,
    gate_in,
    step_size,
    input_proj,
    output_proj,
    decay_log,
    skip_gain,
    out_weight,
    residual,
    routes,
    norm_gain,
    w_gate,
    w_up,
    w_down,
):
    length, channels = mamba_in.shape
    scan = scanned if channels % 128 == 0 else scanned_small
    gated_out = scan(
        mamba_in, gate_in, step_size, input_proj, output_proj, decay_log, skip_gain
    )
    experts = lax.axis_size("exp")
    top_count = routes.shape[1]
    capacity = length * top_count * 2 // experts
    row_ids = route_rows(routes, capacity, experts)
    rows_here = capacity // lax.axis_size("tp")
    col_width = residual.shape[1]
    model_width = out_weight.shape[1]
    offset = lax.axis_index(("exp", "tp")) * col_width
    mixed_rows = jnp.dot(gated_out, out_weight, preferred_element_type=jnp.float32)
    lifted = residual.astype(jnp.float32)
    placed = jnp.zeros((lifted.shape[0], model_width), jnp.float32)
    token_part = lax.psum_scatter(
        mixed_rows + lax.dynamic_update_slice_in_dim(placed, lifted, offset, 1),
        ("exp", "tp"),
        scatter_dimension=0,
        tiled=True,
    )
    every_token = lax.all_gather(
        rms_scale(token_part, norm_gain), ("exp", "tp"), axis=0, tiled=True
    )
    picker = pick_rows(row_ids, lax.axis_index(("exp", "tp")) * rows_here, rows_here)
    normed = jnp.dot(picker, every_token, preferred_element_type=jnp.float32).astype(jnp.bfloat16)
    row_block = lax.all_gather(normed, ("ctx", "tp"), axis=0, tiled=True)
    gate_part = jnp.dot(row_block, w_gate[0], preferred_element_type=jnp.float32)
    up_part = jnp.dot(row_block, w_up[0], preferred_element_type=jnp.float32)
    hidden = (jax.nn.silu(gate_part) * up_part).astype(jnp.bfloat16)
    local_down = w_down[0]
    partial_out = jnp.dot(
        lax.all_gather(hidden, "tp", axis=1, tiled=True),
        local_down,
        preferred_element_type=jnp.float32,
    )
    result = lax.psum_scatter(
        partial_out.astype(jnp.bfloat16), "ctx", scatter_dimension=0, tiled=True
    )
    return result[None, None]


def solution(mesh):
    in_specs = (
        P("ctx", ("exp", "tp")),
        P("ctx", ("exp", "tp")),
        P("ctx", ("exp", "tp")),
        P(None, "ctx"),
        P(None, "ctx"),
        P(None, ("exp", "tp")),
        P(("exp", "tp")),
        P(("exp", "tp"), None),
        P("ctx", ("exp", "tp")),
        P("ctx", None),
        P(),
        P("exp", None, ("ctx", "tp")),
        P("exp", None, ("ctx", "tp")),
        P("exp", "ctx", "tp"),
    )
    out_specs = P("ctx", "exp", None, "tp")
    return jax.shard_map(body, mesh=mesh, in_specs=in_specs, out_specs=out_specs, check_vma=False)
```

```python
import jax
import jax.numpy as jnp
from jax import lax
from jax.experimental import pallas as pl
from jax.experimental.pallas import tpu as pltpu
from jax.sharding import PartitionSpec as P


def prefix_2(value, axis, join, neutral):
    count, mine = (lax.axis_size(axis), lax.axis_index(axis))
    pieces = jax.tree.map(lambda part: lax.all_gather(part, axis), value)
    so_far = jax.tree.map(
        lambda part, zero: jnp.full_like(part, 0) + jnp.asarray(zero, part.dtype), value, neutral
    )

    def step(position, so_far):
        longer = join(so_far, jax.tree.map(lambda part: part[position], pieces))
        return jax.tree.map(lambda new, old: jnp.where(position < mine, new, old), longer, so_far)

    return lax.fori_loop(0, count - 1, step, so_far)


def route_rows(routes, capacity, experts):
    flattened = routes.reshape(-1)
    one_hot = (flattened[:, None] == jnp.arange(experts, dtype=jnp.int32)[None, :]).astype(
        jnp.int32
    )
    earlier = jnp.cumsum(one_hot, axis=0) - one_hot
    slot_index = jnp.sum(earlier * one_hot, axis=1)
    return (flattened * capacity + slot_index).reshape(routes.shape)


def pick_rows(row_ids, first_row, row_count):
    targets = first_row + jnp.arange(row_count, dtype=jnp.int32)
    matches = row_ids[None, :, :] == targets[:, None, None]
    return jnp.sum(matches.astype(jnp.float32), axis=2).astype(jnp.bfloat16)


def rms_scale(row_data, norm_gain):
    mean_sq = jnp.mean(row_data * row_data, axis=1, keepdims=True)
    return (row_data * lax.rsqrt(mean_sq + 1e-06) * norm_gain).astype(jnp.bfloat16)


def combine_link(earlier, later_link):
    return (earlier[0] * later_link[0], later_link[0] * earlier[1] + later_link[1])


def fold_states(rates, states, step, drive, in_ref, t):
    return tuple(
        jnp.exp(step * rate) * state + drive * in_ref[n, t]
        for n, (rate, state) in enumerate(zip(rates, states))
    )


def end_kernel(step_ref, drive_ref, rate_ref, in_ref, end_ref):
    count = rate_ref.shape[0]
    rates = [rate_ref[n] for n in range(count)]

    def advance(t, carried):
        states, total = carried
        step = step_ref[t]
        return (fold_states(rates, states, step, drive_ref[t], in_ref, t), total + step)

    zero = jnp.zeros(rate_ref.shape[1:], jnp.float32)
    states, total = lax.fori_loop(
        0, step_ref.shape[0], advance, ((zero,) * count, zero), unroll=4
    )
    for n in range(count):
        end_ref[n] = states[n]
    end_ref[count] = total


def read_kernel(
    step_ref, drive_ref, signal_ref, gate_ref, skip_ref, rate_ref, ends_ref, in_ref, out_ref, res_ref
):
    count = rate_ref.shape[0]
    mine = lax.axis_index("ctx")
    rates = [rate_ref[n] for n in range(count)]
    zero = jnp.zeros(rate_ref.shape[1:], jnp.float32)

    def join(block, states):
        total = ends_ref[block, count]
        return tuple(
            jnp.exp(total * rates[n]) * states[n] + ends_ref[block, n] for n in range(count)
        )

    incoming = lax.fori_loop(0, mine, join, (zero,) * count)
    skip = skip_ref[...]

    def advance(t, states):
        states = fold_states(rates, states, step_ref[t], drive_ref[t], in_ref, t)
        terms = [states[n] * out_ref[n, t] for n in range(count)]
        while len(terms) > 1:
            terms = [terms[i] + terms[i + 1] for i in range(0, len(terms), 2)]
        gate = gate_ref[t]
        res_ref[t] = (terms[0] + skip * signal_ref[t]) * (gate / (1.0 + jnp.exp(-gate)))
        return states

    lax.fori_loop(0, step_ref.shape[0], advance, incoming, unroll=4)


def scanned(mamba_in, gate_in, step_size, input_proj, output_proj, decay_log, skip_gain):
    length, channels = mamba_in.shape
    count = decay_log.shape[0]
    tile = (channels // 128, 128)
    signal = mamba_in.astype(jnp.float32).reshape((length,) + tile)
    gate = gate_in.astype(jnp.float32).reshape((length,) + tile)
    step = step_size.reshape((length,) + tile)
    drive = step * signal
    rate = -jnp.exp(decay_log).reshape((count,) + tile)
    vmem = pl.BlockSpec(memory_space=pltpu.VMEM)
    smem = pl.BlockSpec(memory_space=pltpu.SMEM)
    ends = pl.pallas_call(
        end_kernel,
        out_shape=jax.ShapeDtypeStruct((count + 1,) + tile, jnp.float32),
        in_specs=[vmem] * 3 + [smem],
        out_specs=vmem,
        name="end_states",
    )(step, drive, rate, input_proj)
    ends = lax.all_gather(ends, "ctx")
    gated = pl.pallas_call(
        read_kernel,
        out_shape=jax.ShapeDtypeStruct((length,) + tile, jnp.float32),
        in_specs=[vmem] * 7 + [smem] * 2,
        out_specs=vmem,
        name="read_states",
    )(step, drive, signal, gate, skip_gain.reshape(tile), rate, ends, input_proj, output_proj)
    return gated.reshape(length, channels).astype(jnp.bfloat16)


MESH = pl.DeviceIdType.MESH


def greet(peers):
    barrier = pltpu.get_barrier_semaphore()
    for peer in peers:
        pl.semaphore_signal(barrier, inc=1, device_id=peer, device_id_type=MESH)
    pl.semaphore_wait(barrier, len(peers))


def expert_steps(rows_ref, out_ref, weights, wd_copy, bufs, sems):
    wg, wu, wd, gate_copy, up_copy = weights
    own, other, acc, part, inbox = bufs
    h_send, h_recv, r_send, r_recv = sems
    ctx, tp = lax.axis_index("ctx"), lax.axis_index("tp")
    blocks, capacity, depth = rows_ref.shape
    chunks, tiles, _, width = own.shape
    piece = capacity // chunks

    def hidden_copy(j, k):
        return pltpu.make_async_remote_copy(
            src_ref=own.at[j, k],
            dst_ref=other.at[j, k],
            send_sem=h_send.at[j, k],
            recv_sem=h_recv.at[j, k],
            device_id={"tp": 1 - tp},
            device_id_type=MESH,
        )

    def part_copy(j, d):
        target = lax.rem(ctx + d, blocks)
        return pltpu.make_async_remote_copy(
            src_ref=part.at[j, target],
            dst_ref=inbox.at[j, d - 1],
            send_sem=r_send.at[j, d - 1],
            recv_sem=r_recv.at[j, d - 1],
            device_id={"ctx": target},
            device_id_type=MESH,
        )

    for j in range(chunks):

        def hidden_step(k, unused, j=j):
            if j == 0:
                gate_copy(k).wait()
                up_copy(k).wait()
            rows = rows_ref[:, pl.ds(j * piece, piece), :].reshape(blocks * piece, depth)
            gate = jnp.dot(rows, wg[k], preferred_element_type=jnp.float32)
            up = jnp.dot(rows, wu[k], preferred_element_type=jnp.float32)
            own[j, k] = (gate / (1.0 + jnp.exp(-gate)) * up).astype(jnp.bfloat16)
            hidden_copy(j, k).start()
            return unused

        lax.fori_loop(0, tiles, hidden_step, 0)
    wd_copy().wait()
    for j in range(chunks):
        acc[...] = jnp.zeros_like(acc)

        def down_step(k, unused, j=j):
            mine = pl.multiple_of((tp * tiles + k) * width, width)
            acc[...] += jnp.dot(
                own[j, k], wd[pl.ds(mine, width), :], preferred_element_type=jnp.float32
            )
            return unused

        def down_step_other(k, unused, j=j):
            hidden_copy(j, k).wait_recv()
            theirs = pl.multiple_of(((1 - tp) * tiles + k) * width, width)
            acc[...] += jnp.dot(
                other[j, k], wd[pl.ds(theirs, width), :], preferred_element_type=jnp.float32
            )
            return unused

        lax.fori_loop(0, tiles, down_step, 0)
        lax.fori_loop(0, tiles, down_step_other, 0)
        part[j] = acc[...].reshape(blocks, piece, acc.shape[1]).astype(jnp.bfloat16)
        for d in range(1, blocks):
            part_copy(j, d).start()
    for j in range(chunks):
        total = part[j, ctx].astype(jnp.float32)
        for d in range(1, blocks):
            part_copy(j, d).wait_recv()
            total = total + inbox[j, d - 1].astype(jnp.float32)
        out_ref[pl.ds(j * piece, piece), :] = total.astype(out_ref.dtype)

    def drain(k, unused):
        for j in range(chunks):
            hidden_copy(j, k).wait_send()
        return unused

    lax.fori_loop(0, tiles, drain, 0)
    for j in range(chunks):
        for d in range(1, blocks):
            part_copy(j, d).wait_send()


def weight_copies(gate_hbm, up_hbm, down_hbm, wg, wu, wd, g_sem, u_sem, d_sem):
    width = wg.shape[2]

    def columns(k):
        return pl.ds(pl.multiple_of(k * width, width), width)

    def gate_copy(k):
        return pltpu.make_async_copy(gate_hbm.at[:, columns(k)], wg.at[k], g_sem.at[k])

    def up_copy(k):
        return pltpu.make_async_copy(up_hbm.at[:, columns(k)], wu.at[k], u_sem.at[k])

    def wd_copy():
        return pltpu.make_async_copy(down_hbm, wd, d_sem)

    return gate_copy, up_copy, wd_copy


def expert_kernel(
    rows_ref, gate_hbm, up_hbm, down_hbm, out_ref,
    wg, wu, wd, own, other, acc, part, inbox,
    g_sem, u_sem, d_sem, h_send, h_recv, r_send, r_recv,
):
    gate_copy, up_copy, wd_copy = weight_copies(
        gate_hbm, up_hbm, down_hbm, wg, wu, wd, g_sem, u_sem, d_sem
    )
    for k in range(wg.shape[0]):
        gate_copy(k).start()
        up_copy(k).start()
    wd_copy().start()
    ctx, tp = lax.axis_index("ctx"), lax.axis_index("tp")
    blocks = rows_ref.shape[0]
    greet([{"tp": 1 - tp}] + [{"ctx": lax.rem(ctx + d, blocks)} for d in range(1, blocks)])
    expert_steps(
        rows_ref, out_ref, (wg, wu, wd, gate_copy, up_copy), wd_copy,
        (own, other, acc, part, inbox), (h_send, h_recv, r_send, r_recv),
    )


def expert_scratch(blocks, capacity, depth, hidden, out_width):
    chunks, width = 4, 256
    tiles = hidden // width
    piece = capacity // chunks
    bf16, dma = jnp.bfloat16, pltpu.SemaphoreType.DMA
    return [
        pltpu.VMEM((tiles, depth, width), bf16),
        pltpu.VMEM((tiles, depth, width), bf16),
        pltpu.VMEM((2 * hidden, out_width), bf16),
        pltpu.VMEM((chunks, tiles, blocks * piece, width), bf16),
        pltpu.VMEM((chunks, tiles, blocks * piece, width), bf16),
        pltpu.VMEM((blocks * piece, out_width), jnp.float32),
        pltpu.VMEM((chunks, blocks, piece, out_width), bf16),
        pltpu.VMEM((chunks, blocks - 1, piece, out_width), bf16),
        dma((tiles,)),
        dma((tiles,)),
        dma,
        dma((chunks, tiles)),
        dma((chunks, tiles)),
        dma((chunks, blocks - 1)),
        dma((chunks, blocks - 1)),
    ]


def experts_tiled(row_block, w_gate, w_up, w_down):
    blocks, capacity, depth = row_block.shape
    vmem, anywhere = pl.BlockSpec(memory_space=pltpu.VMEM), pl.BlockSpec(memory_space=pl.ANY)
    return pl.pallas_call(
        expert_kernel,
        out_shape=jax.ShapeDtypeStruct((capacity, w_down.shape[1]), jnp.bfloat16),
        in_specs=[vmem] + [anywhere] * 3,
        out_specs=vmem,
        scratch_shapes=expert_scratch(
            blocks, capacity, depth, w_gate.shape[1], w_down.shape[1]
        ),
        compiler_params=pltpu.CompilerParams(
            collective_id=0, has_side_effects=True, vmem_limit_bytes=60 << 20
        ),
        name="experts",
    )(row_block, w_gate, w_up, w_down)


def mix_kernel(
    gated_ref, weight_ref, residual_ref, gain_ref, pick_ref, rows_ref,
    mix, inbox, tokens, picks,
    p_send, p_recv, m_send, m_recv, a_send, a_recv, c_send, c_recv,
):
    ctx, exp, tp = lax.axis_index("ctx"), lax.axis_index("exp"), lax.axis_index("tp")
    blocks, experts = lax.axis_size("ctx"), lax.axis_size("exp")
    group = 2 * experts
    place = exp * 2 + tp
    shard, depth = mix.shape[1:]
    width = residual_ref.shape[1]
    across = lax.rem(ctx + 2, blocks)
    partner = ctx + 1 - 2 * lax.rem(ctx, 2)
    line = ctx * 2 + tp

    def member(d):
        other = lax.rem(place + d, group)
        return other, {"exp": other // 2, "tp": lax.rem(other, 2)}

    greet(
        [member(d)[1] for d in range(1, group)]
        + [{"ctx": lax.rem(ctx + d, blocks)} for d in range(1, blocks)]
    )

    def send(src, dst, send_sem, recv_sem, device):
        return pltpu.make_async_remote_copy(
            src_ref=src, dst_ref=dst, send_sem=send_sem, recv_sem=recv_sem,
            device_id=device, device_id_type=MESH,
        )

    pick_copies = [
        send(
            pick_ref, picks.at[ctx], p_send.at[d - 1], p_recv.at[d - 1],
            {"ctx": lax.rem(ctx + d, blocks)},
        )
        for d in range(1, blocks)
    ]
    for copy in pick_copies:
        copy.start()
    picks[ctx] = pick_ref[...]

    lifted = residual_ref[...].astype(jnp.float32)
    for n in range(group):
        columns = slice(n * width, (n + 1) * width)
        mixed = jnp.dot(
            gated_ref[...], weight_ref[:, columns], preferred_element_type=jnp.float32
        )
        mixed = mixed + jnp.where(place == n, lifted, 0.0)
        mix[:, :, columns] = mixed.astype(jnp.bfloat16).reshape(group, shard, width)
    mix_copies = []
    for d in range(1, group):
        other, device = member(d)
        mix_copies.append(
            send(mix.at[other], inbox.at[d - 1], m_send.at[d - 1], m_recv.at[d - 1], device)
        )
    for copy in mix_copies:
        copy.start()
    total = mix[place].astype(jnp.float32)
    for d in range(1, group):
        mix_copies[d - 1].wait_recv()
        total = total + inbox[d - 1].astype(jnp.float32)
    mean_sq = jnp.mean(total * total, axis=1, keepdims=True)
    tokens[line, exp] = (total * lax.rsqrt(mean_sq + 1e-06) * gain_ref[...]).astype(jnp.bfloat16)

    def spread(kind, d, which, device):
        owner = lax.rem(exp - d + experts, experts)
        here = tokens.at[which, owner]
        return send(here, here, a_send.at[kind, d], a_recv.at[kind, d], device)

    def share(kind, d, which):
        owner = lax.rem(exp - d + experts, experts)
        here = tokens.at[which, owner]
        return send(here, here, c_send.at[kind, d], c_recv.at[kind, d], {"ctx": partner})

    started, landed = [], []
    mine = tokens.at[line, exp]
    depth_copies = [
        send(
            mine, mine, a_send.at[0, d], a_recv.at[0, d],
            {"exp": lax.rem(exp + d, experts)},
        )
        for d in range(1, experts)
    ]
    for copy in depth_copies:
        copy.start()
    started += depth_copies
    line_y = ctx * 2 + 1 - tp
    line_x = across * 2 + tp
    line_xy = across * 2 + 1 - tp
    over_y, over_x, over_xy = [], [], []
    for d in range(experts):
        if d > 0:
            depth_copies[d - 1].wait_recv()
        over_y.append(spread(1, d, line, {"tp": 1 - tp}))
        over_x.append(spread(2, d, line, {"ctx": across}))
        near = share(0, d, line)
        for copy in (over_y[d], over_x[d], near):
            copy.start()
        landed.append(near)
    for d in range(experts):
        over_y[d].wait_recv()
        over_xy.append(spread(3, d, line_y, {"ctx": across}))
        near = share(1, d, line_y)
        for copy in (over_xy[d], near):
            copy.start()
        landed.append(near)
        over_x[d].wait_recv()
        near = share(2, d, line_x)
        near.start()
        landed.append(near)
    for d in range(experts):
        over_xy[d].wait_recv()
        near = share(3, d, line_xy)
        near.start()
        landed.append(near)
    for copy in landed:
        copy.wait_recv()
    for copy in pick_copies:
        copy.wait_recv()
    for block in range(blocks):
        rows_ref[block] = jnp.dot(
            picks[block],
            tokens[2 * block : 2 * block + 2].reshape(group * shard, depth),
            preferred_element_type=jnp.float32,
        ).astype(jnp.bfloat16)
    for copy in started + over_y + over_x + over_xy + landed + mix_copies + pick_copies:
        copy.wait_send()


def mixed_slots(gated_out, out_weight, residual, norm_gain, row_ids, capacity):
    blocks, experts = lax.axis_size("ctx"), lax.axis_size("exp")
    length, depth = gated_out.shape[0], out_weight.shape[1]
    group = 2 * experts
    shard = length // group
    pick = pick_rows(row_ids, lax.axis_index("exp") * capacity, capacity)
    pick = pick.reshape(capacity, experts, 2, shard).transpose(0, 2, 1, 3)
    bf16, dma = jnp.bfloat16, pltpu.SemaphoreType.DMA
    vmem = pl.BlockSpec(memory_space=pltpu.VMEM)
    return pl.pallas_call(
        mix_kernel,
        out_shape=jax.ShapeDtypeStruct((blocks, capacity, depth), bf16),
        in_specs=[vmem] * 5,
        out_specs=vmem,
        scratch_shapes=[
            pltpu.VMEM((group, shard, depth), bf16),
            pltpu.VMEM((group - 1, shard, depth), bf16),
            pltpu.VMEM((2 * blocks, experts, shard, depth), bf16),
            pltpu.VMEM((blocks, capacity, length), bf16),
            dma((blocks - 1,)),
            dma((blocks - 1,)),
            dma((group - 1,)),
            dma((group - 1,)),
            dma((4, experts)),
            dma((4, experts)),
            dma((4, experts)),
            dma((4, experts)),
        ],
        compiler_params=pltpu.CompilerParams(
            collective_id=1, has_side_effects=True, vmem_limit_bytes=40 << 20
        ),
        name="mix",
    )(gated_out, out_weight, residual, norm_gain[None, :], pick.reshape(capacity, length))


def scanned_small(mamba_in, gate_in, step_size, input_proj, output_proj, decay_log, skip_gain):
    decay_rate = -jnp.exp(decay_log)
    signal = mamba_in.astype(jnp.float32)
    decays = jnp.exp(step_size[:, None, :] * decay_rate[None, :, :])
    driving = (step_size * signal)[:, None, :] * jnp.transpose(input_proj)[:, :, None]
    cum_decay, local_state = lax.associative_scan(combine_link, (decays, driving), axis=0)
    summary = (cum_decay[-1], local_state[-1])
    identity = (jnp.ones_like(summary[0]), jnp.zeros_like(summary[1]))
    prefix = prefix_2(summary, "ctx", combine_link, identity)
    incoming = prefix[1]
    full_state = local_state + cum_decay * incoming[None, :, :]
    readout = jnp.sum(jnp.transpose(output_proj)[:, :, None] * full_state, axis=1)
    return ((readout + skip_gain * signal) * jax.nn.silu(gate_in.astype(jnp.float32))).astype(
        jnp.bfloat16
    )


def body(
    mamba_in,
    gate_in,
    step_size,
    input_proj,
    output_proj,
    decay_log,
    skip_gain,
    out_weight,
    residual,
    routes,
    norm_gain,
    w_gate,
    w_up,
    w_down,
):
    length, channels = mamba_in.shape
    scan = scanned if channels % 128 == 0 else scanned_small
    gated_out = scan(
        mamba_in, gate_in, step_size, input_proj, output_proj, decay_log, skip_gain
    )
    experts = lax.axis_size("exp")
    top_count = routes.shape[1]
    capacity = length * top_count * 2 // experts
    row_ids = route_rows(routes, capacity, experts)
    shard = length // (experts * lax.axis_size("tp"))
    if (
        lax.axis_size("tp") == 2
        and lax.axis_size("ctx") == 4
        and residual.shape[1] % 128 == 0
        and w_gate.shape[2] % 256 == 0
        and capacity % 64 == 0
        and shard % 16 == 0
    ):
        slots = mixed_slots(gated_out, out_weight, residual, norm_gain, row_ids, capacity)
        return experts_tiled(slots, w_gate[0], w_up[0], w_down[0])[None, None]
    rows_here = capacity // lax.axis_size("tp")
    col_width = residual.shape[1]
    model_width = out_weight.shape[1]
    offset = lax.axis_index(("exp", "tp")) * col_width
    mixed_rows = jnp.dot(gated_out, out_weight, preferred_element_type=jnp.float32)
    lifted = residual.astype(jnp.float32)
    placed = jnp.zeros((lifted.shape[0], model_width), jnp.float32)
    token_part = lax.psum_scatter(
        mixed_rows + lax.dynamic_update_slice_in_dim(placed, lifted, offset, 1),
        ("exp", "tp"),
        scatter_dimension=0,
        tiled=True,
    )
    every_token = lax.all_gather(
        rms_scale(token_part, norm_gain), ("exp", "tp"), axis=0, tiled=True
    )
    picker = pick_rows(row_ids, lax.axis_index(("exp", "tp")) * rows_here, rows_here)
    normed = jnp.dot(picker, every_token, preferred_element_type=jnp.float32).astype(jnp.bfloat16)
    row_block = lax.all_gather(normed, ("ctx", "tp"), axis=0, tiled=True)
    gate_part = jnp.dot(row_block, w_gate[0], preferred_element_type=jnp.float32)
    up_part = jnp.dot(row_block, w_up[0], preferred_element_type=jnp.float32)
    hidden = (jax.nn.silu(gate_part) * up_part).astype(jnp.bfloat16)
    local_down = w_down[0]
    partial_out = jnp.dot(
        lax.all_gather(hidden, "tp", axis=1, tiled=True),
        local_down,
        preferred_element_type=jnp.float32,
    )
    result = lax.psum_scatter(
        partial_out.astype(jnp.bfloat16), "ctx", scatter_dimension=0, tiled=True
    )
    return result[None, None]


def solution(mesh):
    in_specs = (
        P("ctx", ("exp", "tp")),
        P("ctx", ("exp", "tp")),
        P("ctx", ("exp", "tp")),
        P(None, "ctx"),
        P(None, "ctx"),
        P(None, ("exp", "tp")),
        P(("exp", "tp")),
        P(("exp", "tp"), None),
        P("ctx", ("exp", "tp")),
        P("ctx", None),
        P(),
        P("exp", None, ("ctx", "tp")),
        P("exp", None, ("ctx", "tp")),
        P("exp", "ctx", "tp"),
    )
    out_specs = P("ctx", "exp", None, "tp")
    return jax.shard_map(body, mesh=mesh, in_specs=in_specs, out_specs=out_specs, check_vma=False)
```

```python
import jax
import jax.numpy as jnp
from jax import lax
from jax.experimental import pallas as pl
from jax.experimental.pallas import tpu as pltpu
from jax.sharding import PartitionSpec as P


def prefix_2(value, axis, join, neutral):
    count, mine = (lax.axis_size(axis), lax.axis_index(axis))
    pieces = jax.tree.map(lambda part: lax.all_gather(part, axis), value)
    so_far = jax.tree.map(
        lambda part, zero: jnp.full_like(part, 0) + jnp.asarray(zero, part.dtype), value, neutral
    )

    def step(position, so_far):
        longer = join(so_far, jax.tree.map(lambda part: part[position], pieces))
        return jax.tree.map(lambda new, old: jnp.where(position < mine, new, old), longer, so_far)

    return lax.fori_loop(0, count - 1, step, so_far)


def route_rows(routes, capacity, experts):
    flattened = routes.reshape(-1)
    one_hot = (flattened[:, None] == jnp.arange(experts, dtype=jnp.int32)[None, :]).astype(
        jnp.int32
    )
    earlier = jnp.cumsum(one_hot, axis=0) - one_hot
    slot_index = jnp.sum(earlier * one_hot, axis=1)
    return (flattened * capacity + slot_index).reshape(routes.shape)


def pick_rows(row_ids, first_row, row_count):
    targets = first_row + jnp.arange(row_count, dtype=jnp.int32)
    matches = row_ids[None, :, :] == targets[:, None, None]
    return jnp.sum(matches.astype(jnp.float32), axis=2).astype(jnp.bfloat16)


def rms_scale(row_data, norm_gain):
    mean_sq = jnp.mean(row_data * row_data, axis=1, keepdims=True)
    return (row_data * lax.rsqrt(mean_sq + 1e-06) * norm_gain).astype(jnp.bfloat16)


def combine_link(earlier, later_link):
    return (earlier[0] * later_link[0], later_link[0] * earlier[1] + later_link[1])


def fold_states(rates, states, step, drive, in_ref, t):
    return tuple(
        jnp.exp(step * rate) * state + drive * in_ref[n, t]
        for n, (rate, state) in enumerate(zip(rates, states))
    )


def end_kernel(step_ref, drive_ref, rate_ref, in_ref, end_ref):
    count = rate_ref.shape[0]
    rates = [rate_ref[n] for n in range(count)]

    def advance(t, carried):
        states, total = carried
        step = step_ref[t]
        return (fold_states(rates, states, step, drive_ref[t], in_ref, t), total + step)

    zero = jnp.zeros(rate_ref.shape[1:], jnp.float32)
    states, total = lax.fori_loop(
        0, step_ref.shape[0], advance, ((zero,) * count, zero), unroll=4
    )
    for n in range(count):
        end_ref[n] = states[n]
    end_ref[count] = total


def read_kernel(
    step_ref, drive_ref, signal_ref, gate_ref, skip_ref, rate_ref, ends_ref, in_ref, out_ref, res_ref
):
    count = rate_ref.shape[0]
    mine = lax.axis_index("ctx")
    rates = [rate_ref[n] for n in range(count)]
    zero = jnp.zeros(rate_ref.shape[1:], jnp.float32)

    def join(block, states):
        total = ends_ref[block, count]
        return tuple(
            jnp.exp(total * rates[n]) * states[n] + ends_ref[block, n] for n in range(count)
        )

    incoming = lax.fori_loop(0, mine, join, (zero,) * count)
    skip = skip_ref[...]

    def advance(t, states):
        states = fold_states(rates, states, step_ref[t], drive_ref[t], in_ref, t)
        terms = [states[n] * out_ref[n, t] for n in range(count)]
        while len(terms) > 1:
            terms = [terms[i] + terms[i + 1] for i in range(0, len(terms), 2)]
        gate = gate_ref[t]
        res_ref[t] = (terms[0] + skip * signal_ref[t]) * (gate / (1.0 + jnp.exp(-gate)))
        return states

    lax.fori_loop(0, step_ref.shape[0], advance, incoming, unroll=4)


def swap_kernel(end_ref, ends_ref, inbox, s_send, s_recv):
    ctx, blocks = lax.axis_index("ctx"), lax.axis_size("ctx")
    peers = [{"ctx": lax.rem(ctx + d, blocks)} for d in range(1, blocks)]
    greet(peers)
    copies = [
        pltpu.make_async_remote_copy(
            src_ref=end_ref,
            dst_ref=inbox.at[d],
            send_sem=s_send.at[d],
            recv_sem=s_recv.at[d],
            device_id=peer,
            device_id_type=MESH,
        )
        for d, peer in enumerate(peers)
    ]
    for copy in copies:
        copy.start()
    ends_ref[ctx] = end_ref[...]
    for d, copy in enumerate(copies):
        copy.wait_recv()
        ends_ref[lax.rem(ctx - d - 1 + blocks, blocks)] = inbox[d]
    for copy in copies:
        copy.wait_send()


def swapped(ends):
    blocks = lax.axis_size("ctx")
    vmem, dma = pl.BlockSpec(memory_space=pltpu.VMEM), pltpu.SemaphoreType.DMA
    return pl.pallas_call(
        swap_kernel,
        out_shape=jax.ShapeDtypeStruct((blocks,) + ends.shape, ends.dtype),
        in_specs=[vmem],
        out_specs=vmem,
        scratch_shapes=[
            pltpu.VMEM((blocks - 1,) + ends.shape, ends.dtype),
            dma((blocks - 1,)),
            dma((blocks - 1,)),
        ],
        compiler_params=pltpu.CompilerParams(collective_id=2, has_side_effects=True),
        name="swap",
    )(ends)


def scanned(mamba_in, gate_in, step_size, input_proj, output_proj, decay_log, skip_gain):
    length, channels = mamba_in.shape
    count = decay_log.shape[0]
    tile = (channels // 128, 128)
    signal = mamba_in.astype(jnp.float32).reshape((length,) + tile)
    gate = gate_in.astype(jnp.float32).reshape((length,) + tile)
    step = step_size.reshape((length,) + tile)
    drive = step * signal
    rate = -jnp.exp(decay_log).reshape((count,) + tile)
    vmem = pl.BlockSpec(memory_space=pltpu.VMEM)
    smem = pl.BlockSpec(memory_space=pltpu.SMEM)
    ends = pl.pallas_call(
        end_kernel,
        out_shape=jax.ShapeDtypeStruct((count + 1,) + tile, jnp.float32),
        in_specs=[vmem] * 3 + [smem],
        out_specs=vmem,
        name="end_states",
    )(step, drive, rate, input_proj)
    ends = swapped(ends)
    gated = pl.pallas_call(
        read_kernel,
        out_shape=jax.ShapeDtypeStruct((length,) + tile, jnp.float32),
        in_specs=[vmem] * 7 + [smem] * 2,
        out_specs=vmem,
        name="read_states",
    )(step, drive, signal, gate, skip_gain.reshape(tile), rate, ends, input_proj, output_proj)
    return gated.reshape(length, channels).astype(jnp.bfloat16)


MESH = pl.DeviceIdType.MESH


def greet(peers):
    barrier = pltpu.get_barrier_semaphore()
    for peer in peers:
        pl.semaphore_signal(barrier, inc=1, device_id=peer, device_id_type=MESH)
    pl.semaphore_wait(barrier, len(peers))


def expert_steps(rows_ref, out_ref, weights, wd_copy, bufs, sems):
    wg, wu, wd, gate_copy, up_copy = weights
    own, other, acc, part, inbox = bufs
    h_send, h_recv, r_send, r_recv = sems
    ctx, tp = lax.axis_index("ctx"), lax.axis_index("tp")
    blocks, capacity, depth = rows_ref.shape
    chunks, tiles, _, width = own.shape
    piece = capacity // chunks

    def hidden_copy(j, k):
        return pltpu.make_async_remote_copy(
            src_ref=own.at[j, k],
            dst_ref=other.at[j, k],
            send_sem=h_send.at[j, k],
            recv_sem=h_recv.at[j, k],
            device_id={"tp": 1 - tp},
            device_id_type=MESH,
        )

    def part_copy(j, d):
        target = lax.rem(ctx + d, blocks)
        return pltpu.make_async_remote_copy(
            src_ref=part.at[j, target],
            dst_ref=inbox.at[j, d - 1],
            send_sem=r_send.at[j, d - 1],
            recv_sem=r_recv.at[j, d - 1],
            device_id={"ctx": target},
            device_id_type=MESH,
        )

    for j in range(chunks):

        def hidden_step(k, unused, j=j):
            if j == 0:
                gate_copy(k).wait()
                up_copy(k).wait()
            rows = rows_ref[:, pl.ds(j * piece, piece), :].reshape(blocks * piece, depth)
            gate = jnp.dot(rows, wg[k], preferred_element_type=jnp.float32)
            up = jnp.dot(rows, wu[k], preferred_element_type=jnp.float32)
            own[j, k] = (gate / (1.0 + jnp.exp(-gate)) * up).astype(jnp.bfloat16)
            hidden_copy(j, k).start()
            return unused

        lax.fori_loop(0, tiles, hidden_step, 0)
    wd_copy().wait()
    for j in range(chunks):
        acc[...] = jnp.zeros_like(acc)

        def down_step(k, unused, j=j):
            mine = pl.multiple_of((tp * tiles + k) * width, width)
            acc[...] += jnp.dot(
                own[j, k], wd[pl.ds(mine, width), :], preferred_element_type=jnp.float32
            )
            return unused

        def down_step_other(k, unused, j=j):
            hidden_copy(j, k).wait_recv()
            theirs = pl.multiple_of(((1 - tp) * tiles + k) * width, width)
            acc[...] += jnp.dot(
                other[j, k], wd[pl.ds(theirs, width), :], preferred_element_type=jnp.float32
            )
            return unused

        lax.fori_loop(0, tiles, down_step, 0)
        lax.fori_loop(0, tiles, down_step_other, 0)
        part[j] = acc[...].reshape(blocks, piece, acc.shape[1]).astype(jnp.bfloat16)
        for d in range(1, blocks):
            part_copy(j, d).start()
    for j in range(chunks):
        total = part[j, ctx].astype(jnp.float32)
        for d in range(1, blocks):
            part_copy(j, d).wait_recv()
            total = total + inbox[j, d - 1].astype(jnp.float32)
        out_ref[pl.ds(j * piece, piece), :] = total.astype(out_ref.dtype)

    def drain(k, unused):
        for j in range(chunks):
            hidden_copy(j, k).wait_send()
        return unused

    lax.fori_loop(0, tiles, drain, 0)
    for j in range(chunks):
        for d in range(1, blocks):
            part_copy(j, d).wait_send()


def weight_copies(gate_hbm, up_hbm, down_hbm, wg, wu, wd, g_sem, u_sem, d_sem):
    width = wg.shape[2]

    def columns(k):
        return pl.ds(pl.multiple_of(k * width, width), width)

    def gate_copy(k):
        return pltpu.make_async_copy(gate_hbm.at[:, columns(k)], wg.at[k], g_sem.at[k])

    def up_copy(k):
        return pltpu.make_async_copy(up_hbm.at[:, columns(k)], wu.at[k], u_sem.at[k])

    def wd_copy():
        return pltpu.make_async_copy(down_hbm, wd, d_sem)

    return gate_copy, up_copy, wd_copy


def expert_kernel(
    rows_ref, gate_hbm, up_hbm, down_hbm, out_ref,
    wg, wu, wd, own, other, acc, part, inbox,
    g_sem, u_sem, d_sem, h_send, h_recv, r_send, r_recv,
):
    gate_copy, up_copy, wd_copy = weight_copies(
        gate_hbm, up_hbm, down_hbm, wg, wu, wd, g_sem, u_sem, d_sem
    )
    for k in range(wg.shape[0]):
        gate_copy(k).start()
        up_copy(k).start()
    wd_copy().start()
    ctx, tp = lax.axis_index("ctx"), lax.axis_index("tp")
    blocks = rows_ref.shape[0]
    greet([{"tp": 1 - tp}] + [{"ctx": lax.rem(ctx + d, blocks)} for d in range(1, blocks)])
    expert_steps(
        rows_ref, out_ref, (wg, wu, wd, gate_copy, up_copy), wd_copy,
        (own, other, acc, part, inbox), (h_send, h_recv, r_send, r_recv),
    )


def expert_scratch(blocks, capacity, depth, hidden, out_width):
    chunks, width = 4, 256
    tiles = hidden // width
    piece = capacity // chunks
    bf16, dma = jnp.bfloat16, pltpu.SemaphoreType.DMA
    return [
        pltpu.VMEM((tiles, depth, width), bf16),
        pltpu.VMEM((tiles, depth, width), bf16),
        pltpu.VMEM((2 * hidden, out_width), bf16),
        pltpu.VMEM((chunks, tiles, blocks * piece, width), bf16),
        pltpu.VMEM((chunks, tiles, blocks * piece, width), bf16),
        pltpu.VMEM((blocks * piece, out_width), jnp.float32),
        pltpu.VMEM((chunks, blocks, piece, out_width), bf16),
        pltpu.VMEM((chunks, blocks - 1, piece, out_width), bf16),
        dma((tiles,)),
        dma((tiles,)),
        dma,
        dma((chunks, tiles)),
        dma((chunks, tiles)),
        dma((chunks, blocks - 1)),
        dma((chunks, blocks - 1)),
    ]


def experts_tiled(row_block, w_gate, w_up, w_down):
    blocks, capacity, depth = row_block.shape
    vmem, anywhere = pl.BlockSpec(memory_space=pltpu.VMEM), pl.BlockSpec(memory_space=pl.ANY)
    return pl.pallas_call(
        expert_kernel,
        out_shape=jax.ShapeDtypeStruct((capacity, w_down.shape[1]), jnp.bfloat16),
        in_specs=[vmem] + [anywhere] * 3,
        out_specs=vmem,
        scratch_shapes=expert_scratch(
            blocks, capacity, depth, w_gate.shape[1], w_down.shape[1]
        ),
        compiler_params=pltpu.CompilerParams(
            collective_id=0, has_side_effects=True, vmem_limit_bytes=60 << 20
        ),
        name="experts",
    )(row_block, w_gate, w_up, w_down)


def mix_kernel(
    gated_ref, weight_ref, residual_ref, gain_ref, pick_ref, rows_ref,
    mix, inbox, tokens, picks,
    p_send, p_recv, m_send, m_recv, a_send, a_recv, c_send, c_recv,
):
    ctx, exp, tp = lax.axis_index("ctx"), lax.axis_index("exp"), lax.axis_index("tp")
    blocks, experts = lax.axis_size("ctx"), lax.axis_size("exp")
    group = 2 * experts
    place = exp * 2 + tp
    shard, depth = mix.shape[1:]
    width = residual_ref.shape[1]
    across = lax.rem(ctx + 2, blocks)
    partner = ctx + 1 - 2 * lax.rem(ctx, 2)
    line = ctx * 2 + tp

    def member(d):
        other = lax.rem(place + d, group)
        return other, {"exp": other // 2, "tp": lax.rem(other, 2)}

    greet(
        [member(d)[1] for d in range(1, group)]
        + [{"ctx": lax.rem(ctx + d, blocks)} for d in range(1, blocks)]
    )

    def send(src, dst, send_sem, recv_sem, device):
        return pltpu.make_async_remote_copy(
            src_ref=src, dst_ref=dst, send_sem=send_sem, recv_sem=recv_sem,
            device_id=device, device_id_type=MESH,
        )

    pick_copies = [
        send(
            pick_ref, picks.at[ctx], p_send.at[d - 1], p_recv.at[d - 1],
            {"ctx": lax.rem(ctx + d, blocks)},
        )
        for d in range(1, blocks)
    ]
    for copy in pick_copies:
        copy.start()
    picks[ctx] = pick_ref[...]

    lifted = residual_ref[...].astype(jnp.float32)
    for n in range(group):
        columns = slice(n * width, (n + 1) * width)
        mixed = jnp.dot(
            gated_ref[...], weight_ref[:, columns], preferred_element_type=jnp.float32
        )
        mixed = mixed + jnp.where(place == n, lifted, 0.0)
        mix[:, :, columns] = mixed.astype(jnp.bfloat16).reshape(group, shard, width)
    mix_copies = []
    for d in range(1, group):
        other, device = member(d)
        mix_copies.append(
            send(mix.at[other], inbox.at[d - 1], m_send.at[d - 1], m_recv.at[d - 1], device)
        )
    for copy in mix_copies:
        copy.start()
    total = mix[place].astype(jnp.float32)
    for d in range(1, group):
        mix_copies[d - 1].wait_recv()
        total = total + inbox[d - 1].astype(jnp.float32)
    mean_sq = jnp.mean(total * total, axis=1, keepdims=True)
    tokens[line, exp] = (total * lax.rsqrt(mean_sq + 1e-06) * gain_ref[...]).astype(jnp.bfloat16)

    def spread(kind, d, which, device):
        owner = lax.rem(exp - d + experts, experts)
        here = tokens.at[which, owner]
        return send(here, here, a_send.at[kind, d], a_recv.at[kind, d], device)

    def share(kind, d, which):
        owner = lax.rem(exp - d + experts, experts)
        here = tokens.at[which, owner]
        return send(here, here, c_send.at[kind, d], c_recv.at[kind, d], {"ctx": partner})

    started, landed = [], []
    mine = tokens.at[line, exp]
    depth_copies = [
        send(
            mine, mine, a_send.at[0, d], a_recv.at[0, d],
            {"exp": lax.rem(exp + d, experts)},
        )
        for d in range(1, experts)
    ]
    for copy in depth_copies:
        copy.start()
    started += depth_copies
    line_y = ctx * 2 + 1 - tp
    line_x = across * 2 + tp
    line_xy = across * 2 + 1 - tp
    over_y, over_x, over_xy = [], [], []
    for d in range(experts):
        if d > 0:
            depth_copies[d - 1].wait_recv()
        over_y.append(spread(1, d, line, {"tp": 1 - tp}))
        over_x.append(spread(2, d, line, {"ctx": across}))
        near = share(0, d, line)
        for copy in (over_y[d], over_x[d], near):
            copy.start()
        landed.append(near)
    for d in range(experts):
        over_y[d].wait_recv()
        over_xy.append(spread(3, d, line_y, {"ctx": across}))
        near = share(1, d, line_y)
        for copy in (over_xy[d], near):
            copy.start()
        landed.append(near)
        over_x[d].wait_recv()
        near = share(2, d, line_x)
        near.start()
        landed.append(near)
    for d in range(experts):
        over_xy[d].wait_recv()
        near = share(3, d, line_xy)
        near.start()
        landed.append(near)
    for copy in landed:
        copy.wait_recv()
    for copy in pick_copies:
        copy.wait_recv()
    for block in range(blocks):
        rows_ref[block] = jnp.dot(
            picks[block],
            tokens[2 * block : 2 * block + 2].reshape(group * shard, depth),
            preferred_element_type=jnp.float32,
        ).astype(jnp.bfloat16)
    for copy in started + over_y + over_x + over_xy + landed + mix_copies + pick_copies:
        copy.wait_send()


def mixed_slots(gated_out, out_weight, residual, norm_gain, row_ids, capacity):
    blocks, experts = lax.axis_size("ctx"), lax.axis_size("exp")
    length, depth = gated_out.shape[0], out_weight.shape[1]
    group = 2 * experts
    shard = length // group
    pick = pick_rows(row_ids, lax.axis_index("exp") * capacity, capacity)
    pick = pick.reshape(capacity, experts, 2, shard).transpose(0, 2, 1, 3)
    bf16, dma = jnp.bfloat16, pltpu.SemaphoreType.DMA
    vmem = pl.BlockSpec(memory_space=pltpu.VMEM)
    return pl.pallas_call(
        mix_kernel,
        out_shape=jax.ShapeDtypeStruct((blocks, capacity, depth), bf16),
        in_specs=[vmem] * 5,
        out_specs=vmem,
        scratch_shapes=[
            pltpu.VMEM((group, shard, depth), bf16),
            pltpu.VMEM((group - 1, shard, depth), bf16),
            pltpu.VMEM((2 * blocks, experts, shard, depth), bf16),
            pltpu.VMEM((blocks, capacity, length), bf16),
            dma((blocks - 1,)),
            dma((blocks - 1,)),
            dma((group - 1,)),
            dma((group - 1,)),
            dma((4, experts)),
            dma((4, experts)),
            dma((4, experts)),
            dma((4, experts)),
        ],
        compiler_params=pltpu.CompilerParams(
            collective_id=1, has_side_effects=True, vmem_limit_bytes=40 << 20
        ),
        name="mix",
    )(gated_out, out_weight, residual, norm_gain[None, :], pick.reshape(capacity, length))


def scanned_small(mamba_in, gate_in, step_size, input_proj, output_proj, decay_log, skip_gain):
    decay_rate = -jnp.exp(decay_log)
    signal = mamba_in.astype(jnp.float32)
    decays = jnp.exp(step_size[:, None, :] * decay_rate[None, :, :])
    driving = (step_size * signal)[:, None, :] * jnp.transpose(input_proj)[:, :, None]
    cum_decay, local_state = lax.associative_scan(combine_link, (decays, driving), axis=0)
    summary = (cum_decay[-1], local_state[-1])
    identity = (jnp.ones_like(summary[0]), jnp.zeros_like(summary[1]))
    prefix = prefix_2(summary, "ctx", combine_link, identity)
    incoming = prefix[1]
    full_state = local_state + cum_decay * incoming[None, :, :]
    readout = jnp.sum(jnp.transpose(output_proj)[:, :, None] * full_state, axis=1)
    return ((readout + skip_gain * signal) * jax.nn.silu(gate_in.astype(jnp.float32))).astype(
        jnp.bfloat16
    )


def body(
    mamba_in,
    gate_in,
    step_size,
    input_proj,
    output_proj,
    decay_log,
    skip_gain,
    out_weight,
    residual,
    routes,
    norm_gain,
    w_gate,
    w_up,
    w_down,
):
    length, channels = mamba_in.shape
    scan = scanned if channels % 128 == 0 else scanned_small
    gated_out = scan(
        mamba_in, gate_in, step_size, input_proj, output_proj, decay_log, skip_gain
    )
    experts = lax.axis_size("exp")
    top_count = routes.shape[1]
    capacity = length * top_count * 2 // experts
    row_ids = route_rows(routes, capacity, experts)
    shard = length // (experts * lax.axis_size("tp"))
    if (
        lax.axis_size("tp") == 2
        and lax.axis_size("ctx") == 4
        and residual.shape[1] % 128 == 0
        and w_gate.shape[2] % 256 == 0
        and capacity % 64 == 0
        and shard % 16 == 0
    ):
        slots = mixed_slots(gated_out, out_weight, residual, norm_gain, row_ids, capacity)
        return experts_tiled(slots, w_gate[0], w_up[0], w_down[0])[None, None]
    rows_here = capacity // lax.axis_size("tp")
    col_width = residual.shape[1]
    model_width = out_weight.shape[1]
    offset = lax.axis_index(("exp", "tp")) * col_width
    mixed_rows = jnp.dot(gated_out, out_weight, preferred_element_type=jnp.float32)
    lifted = residual.astype(jnp.float32)
    placed = jnp.zeros((lifted.shape[0], model_width), jnp.float32)
    token_part = lax.psum_scatter(
        mixed_rows + lax.dynamic_update_slice_in_dim(placed, lifted, offset, 1),
        ("exp", "tp"),
        scatter_dimension=0,
        tiled=True,
    )
    every_token = lax.all_gather(
        rms_scale(token_part, norm_gain), ("exp", "tp"), axis=0, tiled=True
    )
    picker = pick_rows(row_ids, lax.axis_index(("exp", "tp")) * rows_here, rows_here)
    normed = jnp.dot(picker, every_token, preferred_element_type=jnp.float32).astype(jnp.bfloat16)
    row_block = lax.all_gather(normed, ("ctx", "tp"), axis=0, tiled=True)
    gate_part = jnp.dot(row_block, w_gate[0], preferred_element_type=jnp.float32)
    up_part = jnp.dot(row_block, w_up[0], preferred_element_type=jnp.float32)
    hidden = (jax.nn.silu(gate_part) * up_part).astype(jnp.bfloat16)
    local_down = w_down[0]
    partial_out = jnp.dot(
        lax.all_gather(hidden, "tp", axis=1, tiled=True),
        local_down,
        preferred_element_type=jnp.float32,
    )
    result = lax.psum_scatter(
        partial_out.astype(jnp.bfloat16), "ctx", scatter_dimension=0, tiled=True
    )
    return result[None, None]


def solution(mesh):
    in_specs = (
        P("ctx", ("exp", "tp")),
        P("ctx", ("exp", "tp")),
        P("ctx", ("exp", "tp")),
        P(None, "ctx"),
        P(None, "ctx"),
        P(None, ("exp", "tp")),
        P(("exp", "tp")),
        P(("exp", "tp"), None),
        P("ctx", ("exp", "tp")),
        P("ctx", None),
        P(),
        P("exp", None, ("ctx", "tp")),
        P("exp", None, ("ctx", "tp")),
        P("exp", "ctx", "tp"),
    )
    out_specs = P("ctx", "exp", None, "tp")
    return jax.shard_map(body, mesh=mesh, in_specs=in_specs, out_specs=out_specs, check_vma=False)
```
